32 devices in a mesh: row: 4 (over y, core), col: 8 (over z, x).
Axes of the slice: x: 2, y: 2, z: 4, core: 2. Of those that a mesh axis runs over, the one named last changes fastest.
Arguments:
- node_feats: bfloat16 [8192, 512], P(('row', 'col')), may hold values from -6 to 6
- w_gate: bfloat16 [512, 2048], P(None, ('row', 'col')), may hold values from -0.25 to 0.25
- w_up: bfloat16 [512, 2048], P(None, ('row', 'col')), may hold values from -0.25 to 0.25
- w_down: bfloat16 [2048, 512], P(('row', 'col')), may hold values from -0.125 to 0.125
- tile_src: int32 [512], P(('row', 'col')), may hold values from 0 to 3
- tile_dst: int32 [512], P(('row', 'col')), may hold values from 0 to 1
- tile_mask: int32 [512, 512, 512], P(('row', 'col')), may hold values 0 or 1
- tile_count: int32 [32], P(('row', 'col')), may hold values from 1 to 16, as said below
Outputs:
- entry_loss: float32 [], replicated
- grad_gate: float32 [512, 2048], P(None, ('row', 'col'))
- grad_up: float32 [512, 2048], P(None, ('row', 'col'))
- grad_down: float32 [2048, 512], P(('row', 'col'))
The draws below stay inside these ranges and needn't reach their ends.
Inputs may be any that keep to these rules, and one draw needn't show every extreme that they name: `tile_count`: some device has all 16 slots live.
All inputs are finite; a program needn't handle non-finite values. No bound on the sum of `tile_mask` on one device may be relied on, other than what follows from the above.
Results may differ from the reference program's by a relative error of at most 0.01.
Values may be sent and summed in bfloat16 or wider, within the bound.
A program may use at most 128 MiB of HBM per device.

```python
import math
import jax
import jax.numpy as jnp
import numpy as np
from jax import lax

D = 512
FF = 2048
BLOCK = 512
NODE_DEV = 256
TILE_CAP = 16
NODES = 8192
TILES = 512
SRC_BLOCKS = 4
DST_BLOCKS = 2
N_ROW = 4
N_COL = 8
DEVICES = 32


def draw_tile_count(key, part):
    counts = jax.random.randint(key, (DEVICES,), 1, TILE_CAP + 1)
    return counts.at[0].set(TILE_CAP).astype(jnp.int32)


def touch_ends(drawn, key, least, largest):
    index_at = [jax.random.randint(jax.random.fold_in(key, axis), (), 0, length) for axis, length in enumerate(drawn.shape)]
    main_axis = drawn.shape.index(max(drawn.shape))
    neighbour = index_at[:main_axis] + [(index_at[main_axis] + 1) % drawn.shape[main_axis]] + index_at[main_axis + 1:]
    return drawn.at[tuple(index_at)].set(least).at[tuple(neighbour)].set(largest)


def levels(own_key, shape, pieces, smallest, largest):
    gain = 1.0
    for position, parts in pieces:
        draws = jax.random.uniform(jax.random.fold_in(jax.random.fold_in(own_key, 6), position), (parts,), jnp.float32, smallest / len(pieces), largest / len(pieces))
        gain = gain * jnp.repeat(jnp.exp(draws), shape[position] // parts).reshape((-1,) + (1,) * (len(shape) - 1 - position))
    return gain


def rank_table(amount, skew):
    weights = [(1 << 20) // math.isqrt(grade ** skew) + 1 for grade in range(1, amount + 1)]
    spread = 1 + sum(weights) // (1 << 30)
    return np.cumsum(np.array([max(1, weight // spread) for weight in weights]))


def ranked_ids(key, extent, number_of, slope):
    table = rank_table(number_of, slope)
    ticket = jax.random.randint(jax.random.fold_in(key, 1), extent, 0, int(table[number_of - 1]))
    grade = jnp.searchsorted(jnp.asarray(table, jnp.int32), ticket, side="right")
    return jax.random.permutation(jax.random.fold_in(key, 2), number_of)[grade].astype(jnp.int32)


def noise(stream_key, extent, scale, most, shards=(), held_as=jnp.bfloat16):
    loudness = levels(stream_key, extent, shards, -0.22, 0.18) if shards else 1.0
    array = jax.random.normal(stream_key, extent, jnp.float32) * scale * loudness
    return jnp.minimum(jnp.maximum(array, -most), most).astype(held_as)


def setup_inputs(seed: int = 0) -> dict:
    key_of = jax.random.split(jax.random.key(seed), 9)
    return {
        "node_feats": noise(key_of[0], (NODES, D), 1.0, 6.0, ((0, 32),)),
        "w_gate": noise(key_of[1], (D, FF), D ** -0.5, 0.25, ((1, 32),)),
        "w_up": noise(key_of[2], (D, FF), D ** -0.5, 0.25, ((1, 32),)),
        "w_down": noise(key_of[3], (FF, D), FF ** -0.5, 0.125, ((0, 32),)),
        "tile_src": touch_ends(ranked_ids(key_of[4], (TILES,), SRC_BLOCKS, 2), jax.random.fold_in(key_of[4], 3), 0, SRC_BLOCKS - 1).astype(jnp.int32),
        "tile_dst": touch_ends(ranked_ids(key_of[5], (TILES,), DST_BLOCKS, 1), jax.random.fold_in(key_of[5], 3), 0, DST_BLOCKS - 1).astype(jnp.int32),
        "tile_mask": touch_ends((jax.random.randint(key_of[6], (TILES, BLOCK, BLOCK), 0, 8) < 1).astype(jnp.int32), jax.random.fold_in(key_of[6], 1), 0, 1),
        "tile_count": draw_tile_count(jax.random.fold_in(key_of[8], 71), 0),
    }


def reference(node_feats, w_gate, w_up, w_down, tile_src, tile_dst, tile_mask, tile_count):
    gate_proj = jnp.dot(node_feats, w_gate, preferred_element_type=jnp.float32)
    up_proj = jnp.dot(node_feats, w_up, preferred_element_type=jnp.float32)
    hidden = (jax.nn.silu(gate_proj) * up_proj).astype(jnp.bfloat16)
    embedding = (node_feats.astype(jnp.float32) + jnp.dot(hidden, w_down, preferred_element_type=jnp.float32)).astype(jnp.bfloat16)
    across = embedding.reshape(N_ROW, N_COL, NODE_DEV, D).transpose(1, 0, 2, 3).reshape(NODES, D)
    tiles_live = jnp.sum(tile_count).astype(jnp.float32)
    score_scale = D ** -0.5
    grad_factor = score_scale / tiles_live
    src_span = N_COL * NODE_DEV
    dst_span = N_ROW * NODE_DEV

    def device_step(carry, device):
        loss_sum, src_accum, dst_accum = carry
        row_index = device // N_COL
        col_index = device % N_COL
        src_rows = lax.dynamic_slice_in_dim(embedding, (row_index * src_span).astype(jnp.int32), src_span, 0)
        dst_rows = lax.dynamic_slice_in_dim(across, (col_index * dst_span).astype(jnp.int32), dst_span, 0)
        live_slots = tile_count[device]

        def slot_step(inner, slot):
            loss_part, src_part, dst_part = inner
            tile_id = (device * TILE_CAP + slot).astype(jnp.int32)
            live = (slot < live_slots).astype(jnp.float32)
            src_start = (tile_src[tile_id] * BLOCK).astype(jnp.int32)
            dst_start = (tile_dst[tile_id] * BLOCK).astype(jnp.int32)
            src_block = lax.dynamic_slice_in_dim(src_rows, src_start, BLOCK, 0)
            dst_block = lax.dynamic_slice_in_dim(dst_rows, dst_start, BLOCK, 0)
            scores = lax.dot_general(src_block, dst_block, (((1,), (1,)), ((), ())), preferred_element_type=jnp.float32) * score_scale
            labels = lax.dynamic_index_in_dim(tile_mask, tile_id, 0, keepdims=False).astype(jnp.float32)
            loss_part = loss_part + live * jnp.sum(jax.nn.softplus(scores) - labels * scores)
            score_grad = ((jax.nn.sigmoid(scores) - labels) * grad_factor).astype(jnp.bfloat16)
            src_term = jnp.dot(score_grad, dst_block, preferred_element_type=jnp.float32) * live
            dst_term = lax.dot_general(score_grad, src_block, (((0,), (0,)), ((), ())), preferred_element_type=jnp.float32) * live
            old_src = lax.dynamic_slice_in_dim(src_part, src_start, BLOCK, 0)
            src_part = lax.dynamic_update_slice_in_dim(src_part, old_src + src_term, src_start, 0)
            old_dst = lax.dynamic_slice_in_dim(dst_part, dst_start, BLOCK, 0)
            dst_part = lax.dynamic_update_slice_in_dim(dst_part, old_dst + dst_term, dst_start, 0)
            return (loss_part, src_part, dst_part), None

        start_inner = (jnp.zeros((), jnp.float32), jnp.zeros((src_span, D), jnp.float32), jnp.zeros((dst_span, D), jnp.float32))
        (loss_part, src_part, dst_part), unused = lax.scan(slot_step, start_inner, jnp.arange(TILE_CAP, dtype=jnp.int32))
        src_round = lax.optimization_barrier(src_part.astype(jnp.bfloat16)).astype(jnp.float32)
        dst_round = lax.optimization_barrier(dst_part.astype(jnp.bfloat16)).astype(jnp.float32)
        src_begin = (row_index * src_span).astype(jnp.int32)
        dst_begin = (col_index * dst_span).astype(jnp.int32)
        src_accum = lax.dynamic_update_slice_in_dim(src_accum, lax.dynamic_slice_in_dim(src_accum, src_begin, src_span, 0) + src_round, src_begin, 0)
        dst_accum = lax.dynamic_update_slice_in_dim(dst_accum, lax.dynamic_slice_in_dim(dst_accum, dst_begin, dst_span, 0) + dst_round, dst_begin, 0)
        return (loss_sum + loss_part, src_accum, dst_accum), None

    start_outer = (jnp.zeros((), jnp.float32), jnp.zeros((NODES, D), jnp.float32), jnp.zeros((NODES, D), jnp.float32))
    (loss_sum, src_accum, dst_accum), unused = lax.scan(device_step, start_outer, jnp.arange(N_ROW * N_COL, dtype=jnp.int32))
    dst_back = dst_accum.reshape(N_COL, N_ROW, NODE_DEV, D).transpose(1, 0, 2, 3).reshape(NODES, D)
    embed_grad = (src_accum + dst_back).astype(jnp.bfloat16)
    entry_loss = loss_sum / (tiles_live * BLOCK * BLOCK)
    grad_down = lax.dot_general(hidden, embed_grad, (((0,), (0,)), ((), ())), preferred_element_type=jnp.float32)
    hidden_grad = lax.dot_general(embed_grad, w_down, (((1,), (1,)), ((), ())), preferred_element_type=jnp.float32)
    sig = jax.nn.sigmoid(gate_proj)
    gate_grad = (hidden_grad * up_proj * sig * (1.0 + gate_proj * (1.0 - sig))).astype(jnp.bfloat16)
    up_grad = (hidden_grad * gate_proj * sig).astype(jnp.bfloat16)
    grad_gate = lax.dot_general(node_feats, gate_grad, (((0,), (0,)), ((), ())), preferred_element_type=jnp.float32)
    grad_up = lax.dot_general(node_feats, up_grad, (((0,), (0,)), ((), ())), preferred_element_type=jnp.float32)
    return (entry_loss, grad_gate, grad_up, grad_down)
```

```python
import functools
import math

import jax
import jax.numpy as jnp
from jax import lax
from jax.experimental import pallas as pl
from jax.experimental.pallas import tpu as pltpu
from jax.sharding import PartitionSpec as P

BLOCK = 512
NEAR, WIDE = 0, 1
SPLIT = ((4, NEAR), (4, NEAR), (3, NEAR), (2, NEAR), (3, WIDE))
F32 = jnp.float32
BF16 = jnp.bfloat16
NT = (((1,), (1,)), ((), ()))
TN = (((0,), (0,)), ((), ()))


def dot_nt(a, b):
    return lax.dot_general(a, b, NT, preferred_element_type=F32)


def dot_tn(a, b):
    return lax.dot_general(a, b, TN, preferred_element_type=F32)


def halve(x, op, rows):
    while x.shape[0] > rows:
        half = x.shape[0] // 2
        x = op(x[:half], x[half:])
    return x


def tile_kernel(half_scale, count_ref, src_id, dst_id, src_ref, dst_ref, mask_ref,
                src_out, dst_out, loss_out, src_acc, dst_acc, grad_buf, hinge_acc, log_acc):
    slot = pl.program_id(0)
    width = src_ref.shape[1]

    @pl.when(slot == 0)
    def _():
        src_acc[...] = jnp.zeros_like(src_acc)
        dst_acc[...] = jnp.zeros_like(dst_acc)
        hinge_acc[...] = jnp.zeros_like(hinge_acc)
        log_acc[...] = jnp.zeros_like(log_acc)

    @pl.when(slot < count_ref[0])
    def _():
        src_at = pl.ds(pl.multiple_of(src_id[slot] * BLOCK, BLOCK), BLOCK)
        dst_at = pl.ds(pl.multiple_of(dst_id[slot] * BLOCK, BLOCK), BLOCK)
        dst_block = dst_ref[dst_at, :]
        prods = None
        part = 128
        for lo in range(0, BLOCK, part):
            rows = pl.ds(pl.multiple_of(src_id[slot] * BLOCK + lo, part), part)
            raw = dot_nt(src_ref[rows, :], dst_block)
            sign = jnp.where(mask_ref[0, lo:lo + part, :] == 0, 1.0, -1.0)
            half = jnp.tanh(raw * half_scale)
            grad_buf[lo:lo + part, :] = (half + sign).astype(BF16)
            hinge_acc[...] += halve(jnp.maximum(raw * sign, 0.0), jnp.add, 8)
            prod = halve(1.0 + jnp.abs(half), jnp.multiply, 8)
            prods = prod if prods is None else prods * prod
        log_acc[...] += (BLOCK // 8) * math.log(2.0) - jnp.log(prods)
        grad = grad_buf[...]
        src_acc[src_at, :] += jnp.dot(grad, dst_block, preferred_element_type=F32)
        dst_acc[dst_at, :] += dot_tn(grad, src_ref[src_at, :])

    @pl.when(slot == pl.num_programs(0) - 1)
    def _():
        src_out[...] = src_acc[...].astype(BF16)
        dst_out[...] = dst_acc[...].astype(BF16)
        total = hinge_acc[...] * (2.0 * half_scale) + log_acc[...]
        is_loss = lax.broadcasted_iota(jnp.int32, loss_out.shape, 0) == 0
        loss_out[...] = jnp.where(is_loss, jnp.sum(total, keepdims=True), count_ref[0].astype(F32))


def tiles(src_rows, dst_rows, tile_src, tile_dst, tile_mask, tile_count):
    slots = tile_mask.shape[0]
    width = src_rows.shape[1]
    whole = lambda j, *_: (0, 0)
    return pl.pallas_call(
        functools.partial(tile_kernel, 0.5 * width ** -0.5),
        out_shape=(
            jax.ShapeDtypeStruct(src_rows.shape, BF16),
            jax.ShapeDtypeStruct(dst_rows.shape, BF16),
            jax.ShapeDtypeStruct((8, 128), F32),
        ),
        grid_spec=pltpu.PrefetchScalarGridSpec(
            num_scalar_prefetch=3,
            grid=(slots,),
            in_specs=[
                pl.BlockSpec(src_rows.shape, whole, pipeline_mode=pl.Buffered(1)),
                pl.BlockSpec(dst_rows.shape, whole, pipeline_mode=pl.Buffered(1)),
                pl.BlockSpec((1, BLOCK, BLOCK), lambda j, n, s, d: (jnp.minimum(j, n[0] - 1), 0, 0)),
            ],
            out_specs=[
                pl.BlockSpec(src_rows.shape, whole, pipeline_mode=pl.Buffered(1)),
                pl.BlockSpec(dst_rows.shape, whole, pipeline_mode=pl.Buffered(1)),
                pl.BlockSpec((8, 128), whole),
            ],
            scratch_shapes=[
                pltpu.VMEM(src_rows.shape, F32),
                pltpu.VMEM(dst_rows.shape, F32),
                pltpu.VMEM((BLOCK, BLOCK), BF16),
                pltpu.VMEM((8, BLOCK), F32),
                pltpu.VMEM((8, BLOCK), F32),
            ],
        ),
        compiler_params=pltpu.CompilerParams(vmem_limit_bytes=40 << 20),
        name="tiles",
    )(tile_count, tile_src, tile_dst, src_rows, dst_rows, tile_mask)


def advance(steps):
    return [step for step in steps if next(step, True) is None]


def together(*steps):
    steps = advance(steps)
    while steps:
        yield
        steps = advance(steps)


def finish(*steps):
    for _ in together(*steps):
        pass


def group(axis, n, inner):
    me = lax.axis_index(axis)
    return me, me // inner, lax.rem(me, inner)


def gather_near(axis, n, inner, src, place, send, recv):
    outer = n // inner
    me, at_o, at_i = group(axis, n, inner)

    def line(way, k):
        block = at_o - k if way == 0 else at_o + k
        ahead = me + inner if way == 0 else me - inner
        index = way * (outer - 1) + k
        return pltpu.make_async_remote_copy(
            src_ref=src if k == 0 else place(block * inner + at_i),
            dst_ref=place(me if k == 0 else block * inner + at_i),
            send_sem=send.at[index],
            recv_sem=recv.at[index],
            device_id={axis: ahead},
        )

    def sends(way, k):
        if way == 0:
            return jnp.logical_and(at_o - k >= 0, at_o < outer - 1)
        return jnp.logical_and(at_o + k < outer, at_o > 0)

    def arrived(way, k):
        block = at_o - 1 - k if way == 0 else at_o + 1 + k
        index = way * (outer - 1) + k
        here = place(block * inner + at_i)
        return pltpu.make_async_remote_copy(
            src_ref=here, dst_ref=here, send_sem=send.at[index], recv_sem=recv.at[index], device_id={axis: me}
        )

    def arrives(way, k):
        return at_o - 1 - k >= 0 if way == 0 else at_o + 1 + k < outer

    def across(j, block, slot, own, incoming=False):
        index = 2 * (outer - 1) + (j - 1) * (2 * outer - 1) + slot
        peer = at_o * inner + lax.rem(at_i + j, inner)
        where = place(block * inner + (lax.rem(at_i + inner - j, inner) if incoming else at_i))
        return pltpu.make_async_remote_copy(
            src_ref=src if own else where,
            dst_ref=where,
            send_sem=send.at[index],
            recv_sem=recv.at[index],
            device_id={axis: peer},
        )

    def slots():
        for way in range(2):
            for k in range(outer - 1):
                yield way, k, (at_o - 1 - k if way == 0 else at_o + 1 + k), 1 + way * (outer - 1) + k

    for way in range(2):
        @pl.when(sends(way, 0))
        def _(way=way):
            line(way, 0).start()
    for j in range(1, inner):
        across(j, at_o, 0, True).start()
    yield
    for step in range(outer - 1):
        for way, k, block, slot in slots():
            if k != step:
                continue

            @pl.when(arrives(way, k))
            def _(way=way, k=k, block=block, slot=slot):
                arrived(way, k).wait_recv()
                if k + 1 < outer - 1:
                    @pl.when(sends(way, k + 1))
                    def _():
                        line(way, k + 1).start()
                for j in range(1, inner):
                    across(j, block, slot, False).start()
        yield
    for j in range(1, inner):
        across(j, at_o, 0, True, True).wait_recv()
        across(j, at_o, 0, True).wait_send()
    for way, k, block, slot in slots():
        @pl.when(arrives(way, k))
        def _(block=block, slot=slot):
            for j in range(1, inner):
                across(j, block, slot, False, True).wait_recv()
                across(j, block, slot, False).wait_send()

        @pl.when(sends(way, k))
        def _(way=way, k=k):
            line(way, k).wait_send()


def gather_wide(axis, n, inner, src, place, send, recv):
    outer = n // inner
    me, at_o, at_i = group(axis, n, inner)

    def block(o, j):
        return o * inner + lax.rem(at_i + j, inner)

    def line(way, k, j, incoming=False):
        index = inner - 1 + (way * (outer - 1) + k) * inner + j
        step = k + 1 if incoming else k
        where = place(block(at_o - step if way == 0 else at_o + step, j))
        return pltpu.make_async_remote_copy(
            src_ref=src if k == 0 and j == 0 and not incoming else where,
            dst_ref=where,
            send_sem=send.at[index],
            recv_sem=recv.at[index],
            device_id={axis: me if incoming else me + inner if way == 0 else me - inner},
        )

    def sends(way, k):
        if way == 0:
            return jnp.logical_and(at_o - k >= 0, at_o < outer - 1)
        return jnp.logical_and(at_o + k < outer, at_o > 0)

    def arrives(way, k):
        return at_o - 1 - k >= 0 if way == 0 else at_o + 1 + k < outer

    def across(j, incoming=False):
        where = place(block(at_o, inner - j if incoming else 0))
        return pltpu.make_async_remote_copy(
            src_ref=where if incoming else src,
            dst_ref=where,
            send_sem=send.at[j - 1],
            recv_sem=recv.at[j - 1],
            device_id={axis: block(at_o, j)},
        )

    for j in range(1, inner):
        across(j).start()
    for way in range(2):
        @pl.when(sends(way, 0))
        def _(way=way):
            line(way, 0, 0).start()
    yield
    for j in range(1, inner):
        across(j, True).wait_recv()
        for way in range(2):
            @pl.when(sends(way, 0))
            def _(way=way, j=j):
                line(way, 0, inner - j).start()
    yield
    for k in range(outer - 1):
        for way in range(2):
            @pl.when(arrives(way, k))
            def _(way=way, k=k):
                for j in range(inner):
                    line(way, k, j, True).wait_recv()
                    if k + 1 < outer - 1:
                        @pl.when(sends(way, k + 1))
                        def _(j=j):
                            line(way, k + 1, j).start()
        yield
    for j in range(1, inner):
        across(j).wait_send()
    for way in range(2):
        for k in range(outer - 1):
            @pl.when(sends(way, k))
            def _(way=way, k=k):
                for j in range(inner):
                    line(way, k, j).wait_send()


def gather_sems(n, inner, route=NEAR):
    outer = n // inner
    count = inner - 1 + 2 * (outer - 1) * inner
    if route == NEAR:
        count = 2 * (outer - 1) + (inner - 1) * (2 * outer - 1)
    return [pltpu.SemaphoreType.DMA((count,)), pltpu.SemaphoreType.DMA((count,))]


def gather(route, *args):
    return (gather_near, gather_wide)[route](*args)


def chain_line(axis, n, inner):
    outer = n // inner
    me, at_o, at_i = group(axis, n, inner)

    def exists(way, k):
        return at_o + k < outer if way == 0 else at_o - k >= 0

    def fed(way):
        return at_o > 0 if way == 0 else at_o < outer - 1

    def starts(way):
        return at_o == 0 if way == 0 else at_o == outer - 1

    def block(way, k, j):
        return (at_o + k if way == 0 else at_o - k) * inner + lax.rem(at_i + j, inner)

    return exists, fed, starts, block, (me + inner, me - inner)


def reduce_near(axis, n, inner, place, acc, near, out, inn, send, recv):
    outer = n // inner
    exists, fed, starts, block, ahead = chain_line(axis, n, inner)
    base = (inner - 1) * 2 * outer

    def across(j, way, k):
        index = (j - 1) * 2 * outer + way * outer + k
        return pltpu.make_async_remote_copy(
            src_ref=place(block(way, k, j)),
            dst_ref=near.at[index],
            send_sem=send.at[index],
            recv_sem=recv.at[index],
            device_id={axis: block(0, 0, j)},
        )

    def along(way, k):
        slot = way * outer + k
        return pltpu.make_async_remote_copy(
            src_ref=out.at[slot],
            dst_ref=inn.at[slot - 1],
            send_sem=send.at[base + slot],
            recv_sem=recv.at[base + slot - 1],
            device_id={axis: ahead[way]},
        )

    def arrived(way, k):
        slot = way * outer + k
        return pltpu.make_async_remote_copy(
            src_ref=inn.at[slot],
            dst_ref=inn.at[slot],
            send_sem=send.at[base + slot],
            recv_sem=recv.at[base + slot],
            device_id={axis: block(0, 0, 0)},
        )

    def local(way, k):
        total = place(block(way, k, 0))[...].astype(F32)
        for j in range(1, inner):
            across(j, way, k).wait_recv()
            total = total + near[(j - 1) * 2 * outer + way * outer + k].astype(F32)
        return total

    hops = [(way, k) for k in range(outer - 1, 0, -1) for way in range(2)]
    for way, k in hops:
        @pl.when(exists(way, k))
        def _(way=way, k=k):
            for j in range(1, inner):
                across(j, way, k).start()
        if way == 1:
            yield
    for way, k in hops:
        @pl.when(exists(way, k))
        def _(way=way, k=k):
            slot = way * outer + k
            total = local(way, k)
            if k == outer - 1:
                out[slot] = total.astype(BF16)
            else:
                @pl.when(starts(way))
                def _():
                    out[slot] = total.astype(BF16)

                @pl.when(fed(way))
                def _():
                    arrived(way, k).wait_recv()
                    out[slot] = (total + inn[slot].astype(F32)).astype(BF16)
            along(way, k).start()
        if way == 1 and k == 1:
            for j in range(1, inner):
                across(j, 0, 0).start()
        if way == 1:
            yield
    acc[0] = local(0, 0)
    for way in range(2):
        @pl.when(fed(way))
        def _(way=way):
            arrived(way, 0).wait_recv()
            acc[0] += inn[way * outer].astype(F32)
    for j in range(1, inner):
        across(j, 0, 0).wait_send()
    for way, k in hops:
        @pl.when(exists(way, k))
        def _(way=way, k=k):
            for j in range(1, inner):
                across(j, way, k).wait_send()
            along(way, k).wait_send()


def reduce_wide(axis, n, inner, place, acc, near, out, inn, send, recv):
    outer = n // inner
    exists, fed, starts, block, ahead = chain_line(axis, n, inner)
    base = inner - 1

    def along(way, k, j, first):
        slot = (way * outer + k) * inner + j
        return pltpu.make_async_remote_copy(
            src_ref=place(block(way, k, j)) if first else out.at[slot],
            dst_ref=inn.at[slot - inner],
            send_sem=send.at[base + slot],
            recv_sem=recv.at[base + slot - inner],
            device_id={axis: ahead[way]},
        )

    def arrived(way, k, j):
        slot = (way * outer + k) * inner + j
        return pltpu.make_async_remote_copy(
            src_ref=inn.at[slot],
            dst_ref=inn.at[slot],
            send_sem=send.at[base + slot],
            recv_sem=recv.at[base + slot],
            device_id={axis: block(0, 0, 0)},
        )

    def across(j):
        return pltpu.make_async_remote_copy(
            src_ref=out.at[j],
            dst_ref=near.at[j - 1],
            send_sem=send.at[j - 1],
            recv_sem=recv.at[j - 1],
            device_id={axis: block(0, 0, j)},
        )

    hops = [(way, k) for k in range(outer - 1, 0, -1) for way in range(2)]
    for way, k in hops:
        @pl.when(jnp.logical_and(exists(way, k), starts(way)))
        def _(way=way, k=k):
            for j in range(inner):
                along(way, k, j, True).start()
    yield
    yield
    for way, k in hops:
        if k == outer - 1:
            continue

        @pl.when(jnp.logical_and(exists(way, k), fed(way)))
        def _(way=way, k=k):
            for j in range(inner):
                slot = (way * outer + k) * inner + j
                arrived(way, k, j).wait_recv()
                total = place(block(way, k, j))[...].astype(F32) + inn[slot].astype(F32)
                out[slot] = total.astype(BF16)
                along(way, k, j, False).start()
        if way == 1:
            yield
    for j in range(inner):
        acc[j] = place(block(0, 0, j))[...].astype(F32)
    for way in range(2):
        @pl.when(fed(way))
        def _(way=way):
            for j in range(inner):
                arrived(way, 0, j).wait_recv()
                acc[j] += inn[way * outer * inner + j].astype(F32)
    for j in range(1, inner):
        out[j] = acc[j].astype(BF16)
        across(j).start()
    yield
    for j in range(1, inner):
        across(j).wait_recv()
        acc[0] += near[j - 1].astype(F32)
        across(j).wait_send()
    for way, k in hops:
        for first, test in ((True, starts), (False, fed)):
            if k == outer - 1 and not first:
                continue

            @pl.when(jnp.logical_and(exists(way, k), test(way)))
            def _(way=way, k=k, first=first):
                for j in range(inner):
                    along(way, k, j, first).wait_send()


def reduce(route, *args):
    return (reduce_near, reduce_wide)[route](*args)


def reduce_scratch(n, inner, block, route=NEAR):
    outer = n // inner
    near, slots, sums = (inner - 1) * 2 * outer, 2 * outer, 1
    if route == WIDE:
        near, slots, sums = inner - 1, 2 * outer * inner, inner
    return [
        pltpu.VMEM((sums,) + block, F32),
        pltpu.VMEM((near,) + block, BF16),
        pltpu.VMEM((slots,) + block, BF16),
        pltpu.VMEM((slots,) + block, BF16),
        pltpu.SemaphoreType.DMA((near + slots,)),
        pltpu.SemaphoreType.DMA((near + slots,)),
    ]


def greet(axes):
    barrier = pltpu.get_barrier_semaphore()
    total = 0
    for axis, (n, inner) in axes:
        outer = n // inner
        me, at_o, at_i = group(axis, n, inner)
        for j in range(1, inner):
            pl.semaphore_signal(barrier, inc=1, device_id={axis: at_o * inner + lax.rem(at_i + j, inner)})

        @pl.when(at_o > 0)
        def _():
            pl.semaphore_signal(barrier, inc=1, device_id={axis: me - inner})

        @pl.when(at_o < outer - 1)
        def _():
            pl.semaphore_signal(barrier, inc=1, device_id={axis: me + inner})

        total += inner - 1 + lax.div(at_o + outer - 1, outer) + lax.div(2 * outer - 2 - at_o, outer)
    pl.semaphore_wait(barrier, total)


def spans(size):
    unit = size // sum(count for count, _ in SPLIT)
    at = 0
    for count, route in SPLIT:
        yield at, count * unit, route
        at += count * unit


def ahead(pieces):
    return sorted(pieces, key=lambda piece: -piece[2])


def rows_of(ref, size, at, part):
    return lambda block: ref.at[pl.ds(pl.multiple_of(block * size + at, math.gcd(size, at)), part), :]


def take(scratch, count):
    taken = scratch[:count]
    del scratch[:count]
    return taken


def pick(ref, size, at, part):
    return jnp.concatenate([ref[lo:lo + part, :] for lo in range(at, ref.shape[0], size)], axis=0)


def place_back(ref, size, at, part, value):
    for n, lo in enumerate(range(at, ref.shape[0], size)):
        ref[lo:lo + part, :] = value[n * part:(n + 1) * part, :]


def unit_spans(units):
    return ((0, 0, units, NEAR), (1, 0, units, NEAR), (2, 0, units // 2, WIDE), (2, units // 2, units // 2, NEAR))


def forward_kernel(row, col, gate_ref, up_ref, down_ref, x_ref, src_out, dst_out, feats, down_all, hidden,
                   gate_fac, up_fac, gate_all, up_all, branch, own_sem, *scratch):
    scratch = list(scratch)
    units, size = gate_ref.shape[0], x_ref.shape[0]
    whole = (gate_all, up_all, down_all)
    mine = (gate_ref, up_ref, down_ref)
    at_row, at_col = lax.axis_index("row"), lax.axis_index("col")
    local = [
        pltpu.make_async_copy(mine[kind], rows_of(whole[kind], units, 0, units)(at_col), own_sem.at[kind])
        for kind in range(3)
    ]
    local.append(pltpu.make_async_copy(x_ref, rows_of(feats, size, 0, size)(at_row), own_sem.at[3]))
    for copy in local:
        copy.start()
    greet((("row", row), ("col", col)))
    early, late = [], []
    for kind, at, part, route in unit_spans(units):
        src = mine[kind].at[pl.ds(at, part), :]
        steps = gather(route, "col", *col, src, rows_of(whole[kind], units, at, part), *take(scratch, 2))
        (late if kind == 2 else early).append(steps)
    early.append(gather(NEAR, "row", *row, x_ref, rows_of(feats, size, 0, size), *take(scratch, 2)))
    early, late = advance(early), advance(late)
    while early:
        early, late = advance(early), late and advance(late)
    for copy in local:
        copy.wait()

    @pl.loop(0, row[0])
    def _(n):
        at = pl.ds(pl.multiple_of(n * size, size), size)
        gate = dot_nt(feats[at, :], gate_all[...])
        up = dot_nt(feats[at, :], up_all[...])
        sig = jax.nn.sigmoid(gate)
        silu = gate * sig
        hidden[at, :] = (silu * up).astype(BF16)
        gate_fac[at, :] = up * sig * (1.0 + gate * (1.0 - sig))
        up_fac[at, :] = silu

    finish(*late)

    def chain(at, part, route, sums, col_sems, row_sems):
        value = jnp.dot(pick(hidden, size, at, part), down_all[...], preferred_element_type=F32)
        place_back(branch, size, at, part, value.astype(BF16))
        yield from reduce(NEAR, "row", *row, rows_of(branch, size, at, part), *sums)
        here = rows_of(src_out, size, at, part)(at_col)
        held = rows_of(dst_out, size, at, part)(at_row)
        value = (rows_of(feats, size, at, part)(at_row)[...].astype(F32) + sums[0][0]).astype(BF16)
        here[...] = value
        held[...] = value
        yield from together(
            gather(route, "col", *col, here, rows_of(src_out, size, at, part), *col_sems),
            gather(NEAR, "row", *row, held, rows_of(dst_out, size, at, part), *row_sems),
        )

    finish(*[
        chain(at, part, route, take(scratch, 6), take(scratch, 2), take(scratch, 2))
        for at, part, route in ahead(spans(size))
    ])


def backward_kernel(row, col, factor, src_ref, dst_ref, tot_ref, feats, down_all, hidden, gate_fac, up_fac,
                    loss_out, gate_out, up_out, down_out, grad_all, gate_grad, up_grad, parts, tot_row, tot_col,
                    *scratch):
    scratch = list(scratch)
    size, units = feats.shape[0] // row[0], down_out.shape[0]
    at_row, at_col = lax.axis_index("row"), lax.axis_index("col")
    greet((("row", row), ("col", col)))
    tot_row[at_row] = tot_ref[...]

    def totals(row_sems, col_sems):
        yield from gather(NEAR, "row", *row, tot_row.at[at_row], lambda block: tot_row.at[block], *row_sems)
        total = tot_row[0]
        for n in range(1, row[0]):
            total = total + tot_row[n]
        tot_col[at_col] = total
        yield
        yield from gather(NEAR, "col", *col, tot_col.at[at_col], lambda block: tot_col.at[block], *col_sems)

    def chain(at, part, route, col_refs, row_refs, row_sems):
        yield from together(
            reduce(NEAR, "row", *row, rows_of(dst_ref, size, at, part), *row_refs),
            reduce(route, "col", *col, rows_of(src_ref, size, at, part), *col_refs),
        )
        own = rows_of(grad_all, size, at, part)(at_row)
        own[...] = (row_refs[0][0] + col_refs[0][0]).astype(BF16)
        yield from gather(NEAR, "row", *row, own, rows_of(grad_all, size, at, part), *row_sems)
        hidden_grad = dot_nt(pick(grad_all, size, at, part), down_all[...])
        place_back(gate_grad, size, at, part, (hidden_grad * pick(gate_fac, size, at, part)).astype(BF16))
        place_back(up_grad, size, at, part, (hidden_grad * pick(up_fac, size, at, part)).astype(BF16))

    steps = [
        chain(at, part, route, take(scratch, 6), take(scratch, 6), take(scratch, 2)) for at, part, route in spans(size)
    ]
    steps.append(totals(take(scratch, 2), take(scratch, 2)))
    finish(*steps)

    outs = (gate_out, up_out, down_out)
    running = []
    total = tot_col[0]
    for n in range(1, col[0]):
        total = total + tot_col[n]
    scale = factor / total[1:2, :1]

    def spread(kind, at, part, route, refs):
        yield from reduce(route, "col", *col, rows_of(parts.at[kind], units, at, part), *refs)
        outs[kind][at:at + part, :] = refs[0][0] * scale

    for kind, left, right in ((2, hidden, grad_all), (1, up_grad, feats), (0, gate_grad, feats)):
        parts[kind] = dot_tn(left[...], right[...]).astype(BF16)
        for found, at, part, route in unit_spans(units):
            if found == kind:
                running.append(spread(kind, at, part, route, take(scratch, 6)))
                advance(running[-1:])
    loss_out[...] = jnp.broadcast_to(total[0:1, :] / (total[1:2, :] * BLOCK * BLOCK), loss_out.shape)
    finish(*running)


def per_device(row, col, node_feats, w_gate, w_up, w_down, tile_src, tile_dst, tile_mask, tile_count):
    size, width = node_feats.shape
    units = w_down.shape[0]
    shaped = jax.ShapeDtypeStruct
    vmem, hbm = pl.BlockSpec(memory_space=pltpu.VMEM), pl.BlockSpec(memory_space=pltpu.HBM)
    nodes, wide = row[0] * size, col[0] * units
    weight = pltpu.VMEM((wide, width), BF16)
    pieces = list(spans(size))
    scratch = [weight, weight, pltpu.VMEM((nodes, width), BF16), pltpu.SemaphoreType.DMA((4,))]
    for _, _, _, route in unit_spans(units):
        scratch += gather_sems(*col, route)
    scratch += gather_sems(*row)
    for _, part, route in ahead(pieces):
        scratch += reduce_scratch(*row, (part, width)) + gather_sems(*col, route) + gather_sems(*row)
    src_rows, dst_rows, *saved = pl.pallas_call(
        functools.partial(forward_kernel, row, col),
        out_shape=(
            shaped((col[0] * size, width), BF16),
            shaped((nodes, width), BF16),
            shaped((nodes, width), BF16),
            shaped((wide, width), BF16),
            shaped((nodes, wide), BF16),
            shaped((nodes, wide), F32),
            shaped((nodes, wide), F32),
        ),
        in_specs=[hbm] * 4,
        out_specs=(vmem,) * 7,
        scratch_shapes=scratch,
        compiler_params=pltpu.CompilerParams(collective_id=0, has_side_effects=True, vmem_limit_bytes=32 << 20),
        name="forward",
    )(w_gate.T, w_up.T, w_down, node_feats)
    src_part, dst_part, loss_part = tiles(src_rows, dst_rows, tile_src, tile_dst, tile_mask, tile_count)
    tots = loss_part.shape
    scratch = [pltpu.VMEM((nodes, width), BF16), pltpu.VMEM((nodes, wide), BF16), pltpu.VMEM((nodes, wide), BF16)]
    scratch += [pltpu.VMEM((3, wide, width), BF16), pltpu.VMEM((row[0],) + tots, F32), pltpu.VMEM((col[0],) + tots, F32)]
    for _, part, route in pieces:
        scratch += reduce_scratch(*col, (part, width), route) + reduce_scratch(*row, (part, width)) + gather_sems(*row)
    scratch += gather_sems(*row) + gather_sems(*col)
    for kind in (2, 1, 0):
        for found, _, part, route in unit_spans(units):
            if found == kind:
                scratch += reduce_scratch(*col, (part, width), route)
    loss, gate, up, down = pl.pallas_call(
        functools.partial(backward_kernel, row, col, 0.5 * width ** -0.5),
        out_shape=(shaped(tots, F32),) + (shaped((units, width), F32),) * 3,
        in_specs=[vmem] * 8,
        out_specs=(vmem,) * 4,
        scratch_shapes=scratch,
        compiler_params=pltpu.CompilerParams(collective_id=1, has_side_effects=True, vmem_limit_bytes=44 << 20),
        name="backward",
    )(src_part, dst_part, loss_part, *saved)
    return (loss[0, 0], gate.T, up.T, down)


def solution(mesh):
    both = ("row", "col")
    in_specs = (
        P(both, None),
        P(None, both),
        P(None, both),
        P(both, None),
        P(both),
        P(both),
        P(both, None, None),
        P(both),
    )
    out_specs = (P(), P(None, both), P(None, both), P(both, None))
    row = (mesh.shape["row"], 2)
    col = (mesh.shape["col"], mesh.shape["col"] // 4)
    return jax.shard_map(functools.partial(per_device, row, col), mesh=mesh, in_specs=in_specs, out_specs=out_specs, check_vma=False)
```

```python
import functools
import math

import jax
import jax.numpy as jnp
from jax import lax
from jax.experimental import pallas as pl
from jax.experimental.pallas import tpu as pltpu
from jax.sharding import PartitionSpec as P

BLOCK = 512
NEAR, WIDE = 0, 1
SPLIT = ((4, NEAR), (4, NEAR), (3, NEAR), (2, NEAR), (3, WIDE))
F32 = jnp.float32
BF16 = jnp.bfloat16
NT = (((1,), (1,)), ((), ()))
TN = (((0,), (0,)), ((), ()))


def dot_nt(a, b):
    return lax.dot_general(a, b, NT, preferred_element_type=F32)


def dot_tn(a, b):
    return lax.dot_general(a, b, TN, preferred_element_type=F32)


def halve(x, op, rows):
    while x.shape[0] > rows:
        half = x.shape[0] // 2
        x = op(x[:half], x[half:])
    return x


def tile_kernel(half_scale, count_ref, ids, src_ref, dst_ref, mask_ref,
                src_out, dst_out, loss_out, src_acc, dst_acc, grad_buf, hinge_acc, log_acc):
    slot = pl.program_id(0)
    width = src_ref.shape[1]

    @pl.when(slot == 0)
    def _():
        src_acc[...] = jnp.zeros_like(src_acc)
        dst_acc[...] = jnp.zeros_like(dst_acc)
        hinge_acc[...] = jnp.zeros_like(hinge_acc)
        log_acc[...] = jnp.zeros_like(log_acc)

    @pl.when(slot < count_ref[0])
    def _():
        src_at = pl.ds(pl.multiple_of(ids[0, slot] * BLOCK, BLOCK), BLOCK)
        dst_at = pl.ds(pl.multiple_of(ids[1, slot] * BLOCK, BLOCK), BLOCK)
        dst_block = dst_ref[dst_at, :]
        prods = None
        part = 128
        for lo in range(0, BLOCK, part):
            rows = pl.ds(pl.multiple_of(ids[0, slot] * BLOCK + lo, part), part)
            raw = dot_nt(src_ref[rows, :], dst_block)
            sign = jnp.where(mask_ref[0, lo:lo + part, :] == 0, 1.0, -1.0)
            half = jnp.tanh(raw * half_scale)
            grad_buf[lo:lo + part, :] = (half + sign).astype(BF16)
            hinge_acc[...] += halve(jnp.maximum(raw * sign, 0.0), jnp.add, 8)
            prod = halve(1.0 + jnp.abs(half), jnp.multiply, 8)
            prods = prod if prods is None else prods * prod
        log_acc[...] += (BLOCK // 8) * math.log(2.0) - jnp.log(prods)
        grad = grad_buf[...]
        src_acc[src_at, :] += jnp.dot(grad, dst_block, preferred_element_type=F32)
        dst_acc[dst_at, :] += dot_tn(grad, src_ref[src_at, :])

    @pl.when(slot == pl.num_programs(0) - 1)
    def _():
        src_out[...] = src_acc[...].astype(BF16)
        dst_out[...] = dst_acc[...].astype(BF16)
        total = hinge_acc[...] * (2.0 * half_scale) + log_acc[...]
        is_loss = lax.broadcasted_iota(jnp.int32, loss_out.shape, 0) == 0
        loss_out[...] = jnp.where(is_loss, jnp.sum(total, keepdims=True), count_ref[0].astype(F32))


def tiles(src_rows, dst_rows, tile_src, tile_dst, tile_mask, tile_count):
    slots = tile_mask.shape[0]
    width = src_rows.shape[1]
    whole = lambda j, *_: (0, 0)
    return pl.pallas_call(
        functools.partial(tile_kernel, 0.5 * width ** -0.5),
        out_shape=(
            jax.ShapeDtypeStruct(src_rows.shape, BF16),
            jax.ShapeDtypeStruct(dst_rows.shape, BF16),
            jax.ShapeDtypeStruct((8, 128), F32),
        ),
        grid_spec=pltpu.PrefetchScalarGridSpec(
            num_scalar_prefetch=2,
            grid=(slots,),
            in_specs=[
                pl.BlockSpec(src_rows.shape, whole, pipeline_mode=pl.Buffered(1)),
                pl.BlockSpec(dst_rows.shape, whole, pipeline_mode=pl.Buffered(1)),
                pl.BlockSpec((1, BLOCK, BLOCK), lambda j, n, s: (jnp.minimum(j, n[0] - 1), 0, 0)),
            ],
            out_specs=[
                pl.BlockSpec(src_rows.shape, whole, pipeline_mode=pl.Buffered(1)),
                pl.BlockSpec(dst_rows.shape, whole, pipeline_mode=pl.Buffered(1)),
                pl.BlockSpec((8, 128), whole),
            ],
            scratch_shapes=[
                pltpu.VMEM(src_rows.shape, F32),
                pltpu.VMEM(dst_rows.shape, F32),
                pltpu.VMEM((BLOCK, BLOCK), BF16),
                pltpu.VMEM((8, BLOCK), F32),
                pltpu.VMEM((8, BLOCK), F32),
            ],
        ),
        compiler_params=pltpu.CompilerParams(vmem_limit_bytes=40 << 20),
        name="tiles",
    )(tile_count, jnp.stack((tile_src, tile_dst)), src_rows, dst_rows, tile_mask)


def advance(steps):
    return [step for step in steps if next(step, True) is None]


def together(*steps):
    steps = advance(steps)
    while steps:
        yield
        steps = advance(steps)


def finish(*steps):
    for _ in together(*steps):
        pass


def group(axis, n, inner):
    me = lax.axis_index(axis)
    return me, me // inner, lax.rem(me, inner)


def gather_near(axis, n, inner, src, place, send, recv):
    outer = n // inner
    me, at_o, at_i = group(axis, n, inner)

    def line(way, k):
        block = at_o - k if way == 0 else at_o + k
        ahead = me + inner if way == 0 else me - inner
        index = way * (outer - 1) + k
        return pltpu.make_async_remote_copy(
            src_ref=src if k == 0 else place(block * inner + at_i),
            dst_ref=place(me if k == 0 else block * inner + at_i),
            send_sem=send.at[0],
            recv_sem=recv.at[index],
            device_id={axis: ahead},
        )

    def sends(way, k):
        if way == 0:
            return jnp.logical_and(at_o - k >= 0, at_o < outer - 1)
        return jnp.logical_and(at_o + k < outer, at_o > 0)

    def arrived(way, k):
        block = at_o - 1 - k if way == 0 else at_o + 1 + k
        index = way * (outer - 1) + k
        here = place(block * inner + at_i)
        return pltpu.make_async_remote_copy(
            src_ref=here, dst_ref=here, send_sem=send.at[0], recv_sem=recv.at[index], device_id={axis: me}
        )

    def arrives(way, k):
        return at_o - 1 - k >= 0 if way == 0 else at_o + 1 + k < outer

    def across(j, block, own):
        where = place(block * inner + at_i)
        return pltpu.make_async_remote_copy(
            src_ref=src if own else where,
            dst_ref=where,
            send_sem=send.at[1],
            recv_sem=recv.at[2 * (outer - 1)],
            device_id={axis: at_o * inner + lax.rem(at_i + j, inner)},
        )

    def bulk(count, sent):
        return pltpu.make_async_remote_copy(
            src_ref=place.span(count),
            dst_ref=place.span(count),
            send_sem=send.at[sent],
            recv_sem=recv.at[2 * (outer - 1)],
            device_id={axis: me},
        )

    def slots():
        for way in range(2):
            for k in range(outer - 1):
                yield way, k, (at_o - 1 - k if way == 0 else at_o + 1 + k)

    for way in range(2):
        @pl.when(sends(way, 0))
        def _(way=way):
            line(way, 0).start()
    for j in range(1, inner):
        across(j, at_o, True).start()
    yield
    for step in range(outer - 1):
        for way, k, block in slots():
            if k != step:
                continue

            @pl.when(arrives(way, k))
            def _(way=way, k=k, block=block):
                arrived(way, k).wait_recv()
                if k + 1 < outer - 1:
                    @pl.when(sends(way, k + 1))
                    def _():
                        line(way, k + 1).start()
                for j in range(1, inner):
                    across(j, block, False).start()
        yield
    bulk(outer * (inner - 1), 1).wait_recv()
    bulk(outer * (inner - 1), 1).wait_send()
    wait_line(outer, at_o, lambda count: bulk(count, 0).wait_send())


def wait_line(outer, at_o, wait):
    edge = jnp.logical_or(at_o == 0, at_o == outer - 1)

    @pl.when(edge)
    def _():
        wait(1)

    if outer > 2:
        @pl.when(jnp.logical_not(edge))
        def _():
            wait(outer + 1)


def gather_wide(axis, n, inner, src, place, send, recv):
    outer = n // inner
    me, at_o, at_i = group(axis, n, inner)

    def block(o, j):
        return o * inner + lax.rem(at_i + j, inner)

    def line(way, k, j, incoming=False):
        index = inner - 1 + (way * (outer - 1) + k) * inner + j
        step = k + 1 if incoming else k
        where = place(block(at_o - step if way == 0 else at_o + step, j))
        return pltpu.make_async_remote_copy(
            src_ref=src if k == 0 and j == 0 and not incoming else where,
            dst_ref=where,
            send_sem=send.at[0],
            recv_sem=recv.at[index],
            device_id={axis: me if incoming else me + inner if way == 0 else me - inner},
        )

    def sends(way, k):
        if way == 0:
            return jnp.logical_and(at_o - k >= 0, at_o < outer - 1)
        return jnp.logical_and(at_o + k < outer, at_o > 0)

    def arrives(way, k):
        return at_o - 1 - k >= 0 if way == 0 else at_o + 1 + k < outer

    def across(j, incoming=False):
        where = place(block(at_o, inner - j if incoming else 0))
        return pltpu.make_async_remote_copy(
            src_ref=where if incoming else src,
            dst_ref=where,
            send_sem=send.at[1],
            recv_sem=recv.at[j - 1],
            device_id={axis: block(at_o, j)},
        )

    for j in range(1, inner):
        across(j).start()
    for way in range(2):
        @pl.when(sends(way, 0))
        def _(way=way):
            line(way, 0, 0).start()
    yield
    for j in range(1, inner):
        across(j, True).wait_recv()
        for way in range(2):
            @pl.when(sends(way, 0))
            def _(way=way, j=j):
                line(way, 0, inner - j).start()
    yield
    for k in range(outer - 1):
        for way in range(2):
            @pl.when(arrives(way, k))
            def _(way=way, k=k):
                for j in range(inner):
                    line(way, k, j, True).wait_recv()
                    if k + 1 < outer - 1:
                        @pl.when(sends(way, k + 1))
                        def _(j=j):
                            line(way, k + 1, j).start()
        yield
    def sent(count, sem):
        pltpu.make_async_remote_copy(
            src_ref=place.span(count),
            dst_ref=place.span(count),
            send_sem=send.at[sem],
            recv_sem=recv.at[0],
            device_id={axis: me},
        ).wait_send()

    sent(inner - 1, 1)
    wait_line(outer, at_o, lambda count: sent(count * inner, 0))


def gather_sems(n, inner, route=NEAR):
    outer = n // inner
    count = 2 * (outer - 1) + 1 if route == NEAR else inner - 1 + 2 * (outer - 1) * inner
    return [pltpu.SemaphoreType.DMA((2,)), pltpu.SemaphoreType.DMA((count,))]


def gather(route, *args):
    return (gather_near, gather_wide)[route](*args)


def chain_line(axis, n, inner):
    outer = n // inner
    me, at_o, at_i = group(axis, n, inner)

    def exists(way, k):
        return at_o + k < outer if way == 0 else at_o - k >= 0

    def fed(way):
        return at_o > 0 if way == 0 else at_o < outer - 1

    def starts(way):
        return at_o == 0 if way == 0 else at_o == outer - 1

    def block(way, k, j):
        return (at_o + k if way == 0 else at_o - k) * inner + lax.rem(at_i + j, inner)

    return exists, fed, starts, block, (me + inner, me - inner)


def reduce_near(axis, n, inner, place, acc, near, out, inn, send, recv):
    outer = n // inner
    exists, fed, starts, block, ahead = chain_line(axis, n, inner)
    base = (inner - 1) * (2 * outer - 1)

    def across(j, way, k):
        index = (j - 1) * 2 * outer + way * outer + k
        return pltpu.make_async_remote_copy(
            src_ref=place(block(way, k, j)),
            dst_ref=near.at[index],
            send_sem=send.at[0],
            recv_sem=recv.at[(j - 1) * (2 * outer - 1) + way * (outer - 1) + k],
            device_id={axis: block(0, 0, j)},
        )

    def along(way, k):
        slot = way * outer + k
        return pltpu.make_async_remote_copy(
            src_ref=out.at[slot],
            dst_ref=inn.at[slot - 1],
            send_sem=send.at[0],
            recv_sem=recv.at[base + way * (outer - 1) + k - 1],
            device_id={axis: ahead[way]},
        )

    def arrived(way, k):
        slot = way * outer + k
        return pltpu.make_async_remote_copy(
            src_ref=inn.at[slot],
            dst_ref=inn.at[slot],
            send_sem=send.at[0],
            recv_sem=recv.at[base + way * (outer - 1) + k],
            device_id={axis: block(0, 0, 0)},
        )

    def local(way, k):
        total = place(block(way, k, 0))[...].astype(F32)
        for j in range(1, inner):
            across(j, way, k).wait_recv()
            total = total + near[(j - 1) * 2 * outer + way * outer + k].astype(F32)
        return total

    hops = [(way, k) for k in range(outer - 1, 0, -1) for way in range(2)]
    for way, k in hops:
        @pl.when(exists(way, k))
        def _(way=way, k=k):
            for j in range(1, inner):
                across(j, way, k).start()
        if way == 1:
            yield
    for way, k in hops:
        @pl.when(exists(way, k))
        def _(way=way, k=k):
            slot = way * outer + k
            total = local(way, k)
            if k == outer - 1:
                out[slot] = total.astype(BF16)
            else:
                @pl.when(starts(way))
                def _():
                    out[slot] = total.astype(BF16)

                @pl.when(fed(way))
                def _():
                    arrived(way, k).wait_recv()
                    out[slot] = (total + inn[slot].astype(F32)).astype(BF16)
            along(way, k).start()
        if way == 1 and k == 1:
            for j in range(1, inner):
                across(j, 0, 0).start()
        if way == 1:
            yield
    acc[0] = local(0, 0)
    for way in range(2):
        @pl.when(fed(way))
        def _(way=way):
            arrived(way, 0).wait_recv()
            acc[0] += inn[way * outer].astype(F32)
    drain(axis, block(0, 0, 0), near, (inner - 1) * outer + outer - 1, send, recv)


def drain(axis, me, ref, count, send, recv):
    pltpu.make_async_remote_copy(
        src_ref=ref.at[pl.ds(0, count)],
        dst_ref=ref.at[pl.ds(0, count)],
        send_sem=send.at[0],
        recv_sem=recv.at[0],
        device_id={axis: me},
    ).wait_send()


def reduce_wide(axis, n, inner, place, acc, near, out, inn, send, recv):
    outer = n // inner
    exists, fed, starts, block, ahead = chain_line(axis, n, inner)
    base = inner - 1

    def along(way, k, j, first):
        slot = (way * outer + k) * inner + j
        return pltpu.make_async_remote_copy(
            src_ref=place(block(way, k, j)) if first else out.at[slot],
            dst_ref=inn.at[slot - inner],
            send_sem=send.at[0],
            recv_sem=recv.at[base + (way * (outer - 1) + k - 1) * inner + j],
            device_id={axis: ahead[way]},
        )

    def arrived(way, k, j):
        slot = (way * outer + k) * inner + j
        return pltpu.make_async_remote_copy(
            src_ref=inn.at[slot],
            dst_ref=inn.at[slot],
            send_sem=send.at[0],
            recv_sem=recv.at[base + (way * (outer - 1) + k) * inner + j],
            device_id={axis: block(0, 0, 0)},
        )

    def across(j):
        return pltpu.make_async_remote_copy(
            src_ref=out.at[j],
            dst_ref=near.at[j - 1],
            send_sem=send.at[0],
            recv_sem=recv.at[j - 1],
            device_id={axis: block(0, 0, j)},
        )

    hops = [(way, k) for k in range(outer - 1, 0, -1) for way in range(2)]
    for way, k in hops:
        @pl.when(jnp.logical_and(exists(way, k), starts(way)))
        def _(way=way, k=k):
            for j in range(inner):
                along(way, k, j, True).start()
    yield
    yield
    for way, k in hops:
        if k == outer - 1:
            continue

        @pl.when(jnp.logical_and(exists(way, k), fed(way)))
        def _(way=way, k=k):
            for j in range(inner):
                slot = (way * outer + k) * inner + j
                arrived(way, k, j).wait_recv()
                total = place(block(way, k, j))[...].astype(F32) + inn[slot].astype(F32)
                out[slot] = total.astype(BF16)
                along(way, k, j, False).start()
        if way == 1:
            yield
    for j in range(inner):
        acc[j] = place(block(0, 0, j))[...].astype(F32)
    for way in range(2):
        @pl.when(fed(way))
        def _(way=way):
            for j in range(inner):
                arrived(way, 0, j).wait_recv()
                acc[j] += inn[way * outer * inner + j].astype(F32)
    for j in range(1, inner):
        out[j] = acc[j].astype(BF16)
        across(j).start()
    yield
    for j in range(1, inner):
        across(j).wait_recv()
        acc[0] += near[j - 1].astype(F32)
    drain(axis, block(0, 0, 0), inn, (outer - 1) * inner + inner - 1, send, recv)


def reduce(route, *args):
    return (reduce_near, reduce_wide)[route](*args)


def reduce_scratch(n, inner, block, route=NEAR):
    outer = n // inner
    near, slots, sums, sems = (inner - 1) * 2 * outer, 2 * outer, 1, (inner - 1) * (2 * outer - 1) + 2 * (outer - 1)
    if route == WIDE:
        near, slots, sums, sems = inner - 1, 2 * outer * inner, inner, inner - 1 + 2 * (outer - 1) * inner
    return [
        pltpu.VMEM((sums,) + block, F32),
        pltpu.VMEM((near,) + block, BF16),
        pltpu.VMEM((slots,) + block, BF16),
        pltpu.VMEM((slots,) + block, BF16),
        pltpu.SemaphoreType.DMA((1,)),
        pltpu.SemaphoreType.DMA((sems,)),
    ]


def greet(axes):
    barrier = pltpu.get_barrier_semaphore()
    total = 0
    for axis, (n, inner) in axes:
        outer = n // inner
        me, at_o, at_i = group(axis, n, inner)
        for j in range(1, inner):
            pl.semaphore_signal(barrier, inc=1, device_id={axis: at_o * inner + lax.rem(at_i + j, inner)})

        @pl.when(at_o > 0)
        def _():
            pl.semaphore_signal(barrier, inc=1, device_id={axis: me - inner})

        @pl.when(at_o < outer - 1)
        def _():
            pl.semaphore_signal(barrier, inc=1, device_id={axis: me + inner})

        total += inner - 1 + lax.div(at_o + outer - 1, outer) + lax.div(2 * outer - 2 - at_o, outer)
    pl.semaphore_wait(barrier, total)


def spans(size):
    unit = size // sum(count for count, _ in SPLIT)
    at = 0
    for count, route in SPLIT:
        yield at, count * unit, route
        at += count * unit


def ahead(pieces):
    return sorted(pieces, key=lambda piece: -piece[2])


class rows_of:
    def __init__(self, ref, size, at, part):
        self.ref, self.size, self.at, self.part = ref, size, at, part

    def __call__(self, block):
        at = pl.multiple_of(block * self.size + self.at, math.gcd(self.size, self.at))
        return self.ref.at[pl.ds(at, self.part), :]

    def span(self, count):
        return self.ref.at[pl.ds(0, count * self.part), :]


class slots_of:
    def __init__(self, ref):
        self.ref = ref

    def __call__(self, block):
        return self.ref.at[block]

    def span(self, count):
        return self.ref.at[pl.ds(0, count)]


def take(scratch, count):
    taken = scratch[:count]
    del scratch[:count]
    return taken


def pick(ref, size, at, part):
    return jnp.concatenate([ref[lo:lo + part, :] for lo in range(at, ref.shape[0], size)], axis=0)


def place_back(ref, size, at, part, value):
    for n, lo in enumerate(range(at, ref.shape[0], size)):
        ref[lo:lo + part, :] = value[n * part:(n + 1) * part, :]


def unit_spans(units):
    return ((0, 0, units, NEAR), (1, 0, units, NEAR), (2, 0, units // 2, WIDE), (2, units // 2, units // 2, NEAR))


def forward_kernel(row, col, units, in_ref, src_out, dst_out, feats, down_all, hidden,
                   gate_fac, up_fac, gate_all, up_all, branch, own_sem, *scratch):
    scratch = list(scratch)
    size = in_ref.shape[0] - 3 * units
    x_ref = in_ref.at[pl.ds(0, size), :]
    whole = (gate_all, up_all, down_all)
    mine = [in_ref.at[pl.ds(size + kind * units, units), :] for kind in range(3)]
    at_row, at_col = lax.axis_index("row"), lax.axis_index("col")
    local = [
        pltpu.make_async_copy(mine[kind], rows_of(whole[kind], units, 0, units)(at_col), own_sem.at[kind])
        for kind in range(3)
    ]
    local.append(pltpu.make_async_copy(x_ref, rows_of(feats, size, 0, size)(at_row), own_sem.at[3]))
    for copy in local:
        copy.start()
    greet((("row", row), ("col", col)))
    early, late = [], []
    for kind, at, part, route in unit_spans(units):
        src = in_ref.at[pl.ds(size + kind * units + at, part), :]
        steps = gather(route, "col", *col, src, rows_of(whole[kind], units, at, part), *take(scratch, 2))
        (late if kind == 2 else early).append(steps)
    early.append(gather(NEAR, "row", *row, x_ref, rows_of(feats, size, 0, size), *take(scratch, 2)))
    early, late = advance(early), advance(late)
    while early:
        early, late = advance(early), late and advance(late)
    for copy in local:
        copy.wait()

    @pl.loop(0, row[0])
    def _(n):
        at = pl.ds(pl.multiple_of(n * size, size), size)
        gate = dot_nt(feats[at, :], gate_all[...])
        up = dot_nt(feats[at, :], up_all[...])
        sig = jax.nn.sigmoid(gate)
        silu = gate * sig
        hidden[at, :] = (silu * up).astype(BF16)
        gate_fac[at, :] = up * sig * (1.0 + gate * (1.0 - sig))
        up_fac[at, :] = silu

    finish(*late)

    def chain(at, part, route, sums, col_sems, row_sems):
        value = jnp.dot(pick(hidden, size, at, part), down_all[...], preferred_element_type=F32)
        place_back(branch, size, at, part, value.astype(BF16))
        yield from reduce(NEAR, "row", *row, rows_of(branch, size, at, part), *sums)
        here = rows_of(src_out, size, at, part)(at_col)
        held = rows_of(dst_out, size, at, part)(at_row)
        value = (rows_of(feats, size, at, part)(at_row)[...].astype(F32) + sums[0][0]).astype(BF16)
        here[...] = value
        held[...] = value
        yield from together(
            gather(route, "col", *col, here, rows_of(src_out, size, at, part), *col_sems),
            gather(NEAR, "row", *row, held, rows_of(dst_out, size, at, part), *row_sems),
        )

    finish(*[
        chain(at, part, route, take(scratch, 6), take(scratch, 2), take(scratch, 2))
        for at, part, route in ahead(spans(size))
    ])


def backward_kernel(row, col, factor, src_ref, dst_ref, tot_ref, feats, down_all, hidden, gate_fac, up_fac,
                    loss_out, gate_out, up_out, down_out, grad_all, gate_grad, up_grad, parts, tot_row, tot_col,
                    *scratch):
    scratch = list(scratch)
    size, units = feats.shape[0] // row[0], down_out.shape[0]
    at_row, at_col = lax.axis_index("row"), lax.axis_index("col")
    greet((("row", row), ("col", col)))
    tot_row[at_row] = tot_ref[...]

    def totals(row_sems, col_sems):
        yield from gather(NEAR, "row", *row, tot_row.at[at_row], slots_of(tot_row), *row_sems)
        total = tot_row[0]
        for n in range(1, row[0]):
            total = total + tot_row[n]
        tot_col[at_col] = total
        yield
        yield from gather(NEAR, "col", *col, tot_col.at[at_col], slots_of(tot_col), *col_sems)

    def chain(at, part, route, col_refs, row_refs, row_sems):
        yield from together(
            reduce(NEAR, "row", *row, rows_of(dst_ref, size, at, part), *row_refs),
            reduce(route, "col", *col, rows_of(src_ref, size, at, part), *col_refs),
        )
        own = rows_of(grad_all, size, at, part)(at_row)
        own[...] = (row_refs[0][0] + col_refs[0][0]).astype(BF16)
        yield from gather(NEAR, "row", *row, own, rows_of(grad_all, size, at, part), *row_sems)
        hidden_grad = dot_nt(pick(grad_all, size, at, part), down_all[...])
        place_back(gate_grad, size, at, part, (hidden_grad * pick(gate_fac, size, at, part)).astype(BF16))
        place_back(up_grad, size, at, part, (hidden_grad * pick(up_fac, size, at, part)).astype(BF16))

    steps = [
        chain(at, part, route, take(scratch, 6), take(scratch, 6), take(scratch, 2)) for at, part, route in spans(size)
    ]
    steps.append(totals(take(scratch, 2), take(scratch, 2)))
    finish(*steps)

    outs = (gate_out, up_out, down_out)
    running = []
    total = tot_col[0]
    for n in range(1, col[0]):
        total = total + tot_col[n]
    scale = factor / total[1:2, :1]

    def spread(kind, at, part, route, refs):
        yield from reduce(route, "col", *col, rows_of(parts.at[kind], units, at, part), *refs)
        outs[kind][at:at + part, :] = refs[0][0] * scale

    for kind, left, right in ((2, hidden, grad_all), (1, up_grad, feats), (0, gate_grad, feats)):
        parts[kind] = dot_tn(left[...], right[...]).astype(BF16)
        for found, at, part, route in unit_spans(units):
            if found == kind:
                running.append(spread(kind, at, part, route, take(scratch, 6)))
                advance(running[-1:])
    loss_out[...] = jnp.broadcast_to(total[0:1, :] / (total[1:2, :] * BLOCK * BLOCK), loss_out.shape)
    finish(*running)


def last_kernel(loss_ref, gate_ref, up_ref, down_ref, loss_out, gate_out, up_out, down_out, sems):
    copies = [
        pltpu.make_async_copy(src, dst, sems.at[n])
        for n, (src, dst) in enumerate(((gate_ref, gate_out), (up_ref, up_out), (down_ref, down_out)))
    ]
    for copy in copies:
        copy.start()
    loss_out[0, 0] = jnp.max(loss_ref[...])
    for copy in copies:
        copy.wait()


def per_device(row, col, node_feats, w_gate, w_up, w_down, tile_src, tile_dst, tile_mask, tile_count):
    size, width = node_feats.shape
    units = w_down.shape[0]
    shaped = jax.ShapeDtypeStruct
    vmem, hbm = pl.BlockSpec(memory_space=pltpu.VMEM), pl.BlockSpec(memory_space=pltpu.HBM)
    nodes, wide = row[0] * size, col[0] * units
    weight = pltpu.VMEM((wide, width), BF16)
    pieces = list(spans(size))
    scratch = [weight, weight, pltpu.VMEM((nodes, width), BF16), pltpu.SemaphoreType.DMA((4,))]
    for _, _, _, route in unit_spans(units):
        scratch += gather_sems(*col, route)
    scratch += gather_sems(*row)
    for _, part, route in ahead(pieces):
        scratch += reduce_scratch(*row, (part, width)) + gather_sems(*col, route) + gather_sems(*row)
    src_rows, dst_rows, *saved = pl.pallas_call(
        functools.partial(forward_kernel, row, col, units),
        out_shape=(
            shaped((col[0] * size, width), BF16),
            shaped((nodes, width), BF16),
            shaped((nodes, width), BF16),
            shaped((wide, width), BF16),
            shaped((nodes, wide), BF16),
            shaped((nodes, wide), F32),
            shaped((nodes, wide), F32),
        ),
        in_specs=[vmem],
        out_specs=(vmem,) * 7,
        scratch_shapes=scratch,
        compiler_params=pltpu.CompilerParams(collective_id=0, has_side_effects=True, vmem_limit_bytes=32 << 20),
        name="forward",
    )(jnp.concatenate((node_feats, w_gate.T, w_up.T, w_down)))
    src_part, dst_part, loss_part = tiles(src_rows, dst_rows, tile_src, tile_dst, tile_mask, tile_count)
    tots = loss_part.shape
    scratch = [pltpu.VMEM((nodes, width), BF16), pltpu.VMEM((nodes, wide), BF16), pltpu.VMEM((nodes, wide), BF16)]
    scratch += [pltpu.VMEM((3, wide, width), BF16), pltpu.VMEM((row[0],) + tots, F32), pltpu.VMEM((col[0],) + tots, F32)]
    for _, part, route in pieces:
        scratch += reduce_scratch(*col, (part, width), route) + reduce_scratch(*row, (part, width)) + gather_sems(*row)
    scratch += gather_sems(*row) + gather_sems(*col)
    for kind in (2, 1, 0):
        for found, _, part, route in unit_spans(units):
            if found == kind:
                scratch += reduce_scratch(*col, (part, width), route)
    loss, gate, up, down = pl.pallas_call(
        functools.partial(backward_kernel, row, col, 0.5 * width ** -0.5),
        out_shape=(shaped(tots, F32),) + (shaped((units, width), F32),) * 3,
        in_specs=[vmem] * 8,
        out_specs=(vmem,) * 4,
        scratch_shapes=scratch,
        compiler_params=pltpu.CompilerParams(collective_id=1, has_side_effects=True, vmem_limit_bytes=44 << 20),
        name="backward",
    )(src_part, dst_part, loss_part, *saved)
    loss, gate, up, down = pl.pallas_call(
        last_kernel,
        out_shape=(shaped((1, 1), F32),) + (shaped((units, width), F32),) * 3,
        in_specs=[vmem] * 4,
        out_specs=(pl.BlockSpec(memory_space=pltpu.SMEM), hbm, hbm, hbm),
        scratch_shapes=[pltpu.SemaphoreType.DMA((3,))],
        compiler_params=pltpu.CompilerParams(vmem_limit_bytes=2 << 20),
        name="last",
    )(loss, gate, up, down)
    return (loss[0, 0], gate.T, up.T, down)


def solution(mesh):
    both = ("row", "col")
    in_specs = (
        P(both, None),
        P(None, both),
        P(None, both),
        P(both, None),
        P(both),
        P(both),
        P(both, None, None),
        P(both),
    )
    out_specs = (P(), P(None, both), P(None, both), P(both, None))
    row = (mesh.shape["row"], 2)
    col = (mesh.shape["col"], mesh.shape["col"] // 4)
    return jax.shard_map(functools.partial(per_device, row, col), mesh=mesh, in_specs=in_specs, out_specs=out_specs, check_vma=False)
```
